768 devices in a mesh: row: 32 (over y, z_hi, core), col: 24 (over x, z_lo).
Axes of the slice: x: 4, y: 8, z: 12 (z_hi: 2, z_lo: 6; z = z_hi * 6 + z_lo), core: 2. Of those that a mesh axis runs over, the one named last changes fastest.
Arguments:
- a_tiles: bfloat16 [98304, 128, 128], P(('row', 'col')), may hold values from -6 to 6
- a_row: int32 [98304], P(('row', 'col')), may hold values from 0 to 95
- a_col: int32 [98304], P(('row', 'col')), may hold values from 0 to 11
- a_count: int32 [768], P(('row', 'col')), may hold values from 32 to 128
- p_tiles: bfloat16 [3072, 128, 128], P(('row', 'col')), may hold values from -0.5 to 0.5
Outputs:
- coarse_tiles: bfloat16 [1536, 128, 128], P(('row', 'col'))
The draws below stay inside these ranges and needn't reach their ends.
All inputs are finite; a program needn't handle non-finite values.
Results may differ from the reference program's by a relative error of at most 0.0049.
Values may be sent and summed in bfloat16 or wider, within the bound.
A program may use at most 32 MiB of HBM per device.

```python
import jax
import jax.numpy as jnp
from jax import lax

TILE = 128
PB = 4
TD = 128
CT = 2
NB = 3072
N_ROW = 32
N_COL = 24


def draw_a_row(key, part):
    total = N_ROW * N_COL * TD
    upper = N_COL * PB
    values = jax.random.randint(jax.random.fold_in(key, 11), (total,), 0, upper)
    values = values.at[0].set(upper - 1).at[1].set(0)
    return values.astype(jnp.int32)


def draw_a_col(key, part):
    total = N_ROW * N_COL * TD
    upper = 3 * PB
    values = jax.random.randint(jax.random.fold_in(key, 12), (total,), 0, upper)
    values = values.at[0].set(upper - 1).at[1].set(0)
    return values.astype(jnp.int32)


def draw_a_count(key, part):
    divisor = 1 + jax.random.randint(jax.random.fold_in(key, 14), (N_ROW * N_COL,), 0, 4)
    counts = TD // divisor
    counts = counts.at[0].set(TD).at[1].set(TD // 4)
    return counts.astype(jnp.int32)


def steps_of(key, dims, split, least, high):
    loudness, own = 1.0, jax.random.fold_in(key, 6)
    for position, parts in split:
        steps = jnp.exp(jax.random.uniform(jax.random.fold_in(own, position), (parts,), jnp.float32, least / len(split), high / len(split)))
        loudness = loudness * jnp.repeat(steps, dims[position] // parts).reshape([-1 if axis == position else 1 for axis in range(len(dims))])
    return loudness


def noise(key, extent, spread, most, split=(), kind=jnp.bfloat16):
    drawn = spread * jax.random.normal(key, extent, jnp.float32)
    if split:
        drawn = drawn * steps_of(key, extent, split, -0.22, 0.18)
    return jnp.clip(drawn, -most, most).astype(kind)


def setup_inputs(seed: int = 0) -> dict:
    keys = jax.random.split(jax.random.key(seed), 6)
    a_tiles = noise(keys[0], (N_ROW * N_COL * TD, TILE, TILE), 1.0, 6.0, ((0, 768),))
    a_row = draw_a_row(jax.random.fold_in(keys[5], 71), 0)
    a_col = draw_a_col(jax.random.fold_in(keys[5], 71), 0)
    a_count = draw_a_count(jax.random.fold_in(keys[5], 71), 0)
    p_tiles = noise(keys[4], (NB, TILE, TILE), TILE ** -0.5, 0.5, ((0, 768),))
    return dict(a_tiles=a_tiles, a_row=a_row, a_col=a_col, a_count=a_count, p_tiles=p_tiles)


def reference(a_tiles, a_row, a_col, a_count, p_tiles):
    blocks = p_tiles.reshape(N_ROW, N_COL, PB, TILE, TILE)
    coarse_total = 3 * PB * PB

    def group_sum(row_index):
        row_side = lax.dynamic_index_in_dim(blocks, row_index, 0, keepdims=False).reshape(N_COL * PB, TILE, TILE)

        def one_device(col_index, total):
            device = (row_index * N_COL + col_index).astype(jnp.int32)
            neighbours = []
            for shift_value in (-1, 0, 1):
                other = ((row_index + shift_value + N_ROW) % N_ROW).astype(jnp.int32)
                group = lax.dynamic_index_in_dim(blocks, other, 0, keepdims=False)
                neighbours.append(lax.dynamic_index_in_dim(group, col_index.astype(jnp.int32), 0, keepdims=False))
            col_side = jnp.concatenate(neighbours, axis=0)
            start = (device * TD).astype(jnp.int32)
            tiles = lax.dynamic_slice_in_dim(a_tiles, start, TD, 0)
            rows = lax.dynamic_slice_in_dim(a_row, start, TD, 0)
            cols = lax.dynamic_slice_in_dim(a_col, start, TD, 0)
            count = lax.dynamic_index_in_dim(a_count, device, 0, keepdims=False)
            is_live = jnp.arange(TD, dtype=jnp.int32) < count
            slots = ((rows % PB) * (3 * PB) + cols).astype(jnp.int32)
            right = col_side[cols]
            image = jnp.einsum("tij,tjk->tik", tiles.astype(jnp.float32), right.astype(jnp.float32)).astype(jnp.bfloat16)
            left = row_side[rows]
            terms = jnp.einsum("tji,tjk->tik", left.astype(jnp.float32), image.astype(jnp.float32))
            terms = jnp.where(is_live[:, None, None], terms, jnp.float32(0.0))
            return total.at[slots].add(terms)

        empty = jnp.zeros((coarse_total, TILE, TILE), jnp.float32)
        total = lax.fori_loop(jnp.int32(0), jnp.int32(N_COL), one_device, empty)
        return total.astype(jnp.bfloat16)

    result = lax.map(group_sum, jnp.arange(N_ROW, dtype=jnp.int32))
    return result.reshape(N_ROW * N_COL * CT, TILE, TILE)
```

```python
import functools

import jax
import jax.numpy as jnp
from jax import lax
from jax.experimental import pallas as pl
from jax.experimental.pallas import tpu as pltpu
from jax.sharding import PartitionSpec as P

MESH = pl.DeviceIdType.MESH
F32 = jnp.float32
BF16 = jnp.bfloat16
NX, NZ = 4, 6


def kernel_body(
    n_row, pb, slots, width,
    acol_s, arow_s, acount_s, acol_v, arow_v, a_hbm, p_hbm, out_ref,
    abuf, colbuf, rowbuf, img, seg, tabv, tabs,
    sb1, rb1, sb2, rb2, red, zb, zr,
    a_sem, p_sem, t_sem, sh_send, sh_recv,
    z_send, z_recv, x_send, x_recv, y_send, y_recv,
    r1_send, r1_recv, r2_send, r2_recv, q_send, q_recv,
):
    row = lax.axis_index("row")
    col = lax.axis_index("col")
    x = col // NZ
    z = lax.rem(col, NZ)
    nc = 3 * pb
    up = (lax.rem(row + 1, n_row), col)
    down = (lax.rem(row + n_row - 1, n_row), col)
    xr = lax.rem(x + 1, NX)
    xl = lax.rem(x + NX - 1, NX)
    xf = lax.rem(x + 2, NX)
    right = (row, xr * NZ + z)
    left = (row, xl * NZ + z)
    zup = (row, x * NZ + lax.rem(z + 1, NZ))
    zdn = (row, x * NZ + lax.rem(z + NZ - 1, NZ))
    has_up = z < NZ - 1
    has_dn = z > 0

    def remote(src, dst, ssem, rsem, dev):
        return pltpu.make_async_remote_copy(
            src_ref=src, dst_ref=dst, send_sem=ssem, recv_sem=rsem,
            device_id=dev, device_id_type=MESH)

    own = colbuf.at[pl.ds(pb, pb)]
    p_copy = pltpu.make_async_copy(p_hbm, own, p_sem)
    p_copy.start()

    barrier = pltpu.get_barrier_semaphore()
    for dev in (right, left, up, down):
        pl.semaphore_signal(barrier, inc=1, device_id=dev, device_id_type=MESH)

    @pl.when(has_up)
    def _():
        pl.semaphore_signal(barrier, inc=1, device_id=zup, device_id_type=MESH)

    @pl.when(has_dn)
    def _():
        pl.semaphore_signal(barrier, inc=1, device_id=zdn, device_id_type=MESH)

    n_a = 4
    part = slots // n_a
    a_copies = []
    for i in range(n_a):
        c = pltpu.make_async_copy(
            a_hbm.at[pl.ds(i * part, part)], abuf.at[pl.ds(i * part, part)], a_sem.at[i])
        a_copies.append(c)

    p_copy.wait()
    for k in range(pb):
        rowbuf[col * pb + k] = colbuf[pb + k].T
    for c in a_copies:
        c.start()

    pl.semaphore_wait(barrier, 4 + has_up.astype(jnp.int32) + has_dn.astype(jnp.int32))

    def slot(xx, zz):
        return rowbuf.at[pl.ds((xx * NZ + zz) * pb, pb)]

    half = pb // 2

    def slot_half(xx, zz, h):
        return rowbuf.at[pl.ds((xx * NZ + zz) * pb + h * half, half)]

    def z_msg(direction, dist, zz):
        dev = zup if direction == 0 else zdn
        s = slot(x, zz)
        return remote(s, s, z_send.at[direction, dist], z_recv.at[direction, dist + 1], dev)

    def z_in(direction, dist, zz):
        s = slot(x, zz)
        return remote(s, s, z_send.at[direction, dist], z_recv.at[direction, dist], zup)

    def x_msg(direction, j, xx, zz):
        dev = right if direction == 0 else left
        s = slot(xx, zz)
        return remote(s, s, x_send.at[direction, j], x_recv.at[direction, j], dev)

    def y_msg(direction, j, xx, zz):
        dev = right if direction == 0 else left
        s = slot_half(xx, zz, direction)
        return remote(s, s, y_send.at[direction, j], y_recv.at[direction, j], dev)

    def when(cond, fn):
        if cond is None:
            fn()
        else:
            pl.when(cond)(fn)

    def entries(h):
        if h == 0:
            return [(0, z, None)]
        return [(h, z - h, z - h >= 0), (NZ - 1 + h, z + h, z + h < NZ)]

    def z_step(h):
        if h == 0:
            pl.when(has_up)(lambda: z_msg(0, 0, z).start())
            pl.when(has_dn)(lambda: z_msg(1, 0, z).start())
            x_msg(0, 0, x, z).start()
            x_msg(1, 0, x, z).start()
            return
        for side, (j, zz, there) in enumerate(entries(h)):
            def go(side=side, j=j, zz=zz):
                z_in(side, h, zz).wait_recv()
                if h < NZ - 1:
                    more = has_up if side == 0 else has_dn
                    pl.when(more)(lambda: z_msg(side, h, zz).start())
                x_msg(0, j, x, zz).start()
                x_msg(1, j, x, zz).start()
            pl.when(there)(go)

    def x_step(h):
        for j, zz, there in entries(h):
            def go(j=j, zz=zz):
                x_msg(0, j, xl, zz).wait_recv()
                y_msg(0, j, xl, zz).start()
                x_msg(1, j, xr, zz).wait_recv()
                y_msg(1, j, xr, zz).start()
            when(there, go)

    def y_step(h):
        for j, zz, there in entries(h):
            def go(j=j, zz=zz):
                y_msg(0, j, xf, zz).wait_recv()
                y_msg(1, j, xf, zz).wait_recv()
            when(there, go)

    def drain(h):
        for side, (j, zz, there) in enumerate(entries(h)):
            def go(side=side, j=j, zz=zz):
                if h == 0:
                    pl.when(has_up)(lambda: z_msg(0, 0, z).wait_send())
                    pl.when(has_dn)(lambda: z_msg(1, 0, z).wait_send())
                elif h < NZ - 1:
                    more = has_up if side == 0 else has_dn
                    pl.when(more)(lambda: z_msg(side, h, zz).wait_send())
                x_msg(0, j, x, zz).wait_send()
                x_msg(1, j, x, zz).wait_send()
                y_msg(0, j, xl, zz).wait_send()
                y_msg(1, j, xr, zz).wait_send()
            when(there, go)

    to_up = remote(own, colbuf.at[pl.ds(0, pb)], sh_send.at[0], sh_recv.at[0], up)
    to_dn = remote(own, colbuf.at[pl.ds(2 * pb, pb)], sh_send.at[1], sh_recv.at[1], down)

    z_step(0)
    to_up.start()
    to_dn.start()

    lane = lax.broadcasted_iota(jnp.int32, (slots, slots), 1)
    sub = lax.broadcasted_iota(jnp.int32, (slots, slots), 0)
    acol = jnp.broadcast_to(acol_v[...], (slots, slots))
    arow = jnp.broadcast_to(arow_v[...], (slots, slots))
    n_out = nc * pb
    key = jnp.where(lane < acount_s[0], (arow & (pb - 1)) * nc + acol, n_out)
    key_t = key.T
    before = (key_t < key) | ((key_t == key) & (sub < lane))
    rank = jnp.sum(before.astype(jnp.int32), axis=0, keepdims=True)
    rank_t = jnp.broadcast_to(rank, (slots, slots)).T
    hit = rank_t == lane
    order = jnp.sum(jnp.where(hit, sub, 0), axis=0, keepdims=True)
    s_key = jnp.sum(jnp.where(hit, key_t, 0), axis=0, keepdims=True)
    last = jnp.sum((key_t <= lane).astype(jnp.int32), axis=0, keepdims=True) - 1
    some = jnp.sum((key_t == lane).astype(jnp.int32), axis=0, keepdims=True)
    s_key8 = jnp.broadcast_to(s_key, (8, slots))
    prev = pltpu.roll(s_key8, 1, 1)
    lane8 = lax.broadcasted_iota(jnp.int32, (8, slots), 1)
    keep = jnp.where((lane8 > 0) & (prev == s_key8), 1, 0)
    sub8 = lax.broadcasted_iota(jnp.int32, (8, slots), 0)
    tabv[...] = jnp.where(
        sub8 == 0, jnp.broadcast_to(order, (8, slots)),
        jnp.where(sub8 == 1, keep,
                  jnp.where(sub8 == 2, jnp.broadcast_to(jnp.maximum(last, 0), (8, slots)),
                            jnp.broadcast_to(jnp.minimum(some, 1), (8, slots)))))
    t_copy = pltpu.make_async_copy(tabv, tabs, t_sem)
    t_copy.start()

    U = 8

    def images(first, count):
        def body(i, carry):
            for u in range(U):
                t = first + i * U + u
                img[t] = jnp.dot(abuf[t], colbuf[acol_s[t]],
                                 preferred_element_type=F32).astype(BF16)
            return carry
        lax.fori_loop(0, count // U, body, 0)

    z_step(1)
    x_step(0)
    z_step(2)
    x_step(1)
    to_up.wait_recv()
    to_dn.wait_recv()
    for c in a_copies:
        c.wait()
    images(0, 16)
    z_step(3)
    x_step(2)
    images(16, 16)
    z_step(4)
    x_step(3)
    images(32, 16)
    z_step(5)
    x_step(4)
    images(48, 40)
    x_step(5)
    images(88, 40)
    for h in range(NZ):
        y_step(h)
    t_copy.wait()

    def terms(i, carry):
        for u in range(U):
            p = i * U + u
            t = tabs[0, p]
            term = jnp.dot(rowbuf[arow_s[t]], img[t], preferred_element_type=F32)
            carry = carry * tabs[1, p].astype(F32) + term
            seg[p] = carry
        return carry
    lax.fori_loop(0, slots // U, terms, jnp.zeros((width, width), F32))

    def total(s):
        return seg[tabs[2, s]] * tabs[3, s].astype(F32)

    hc = nc // 2

    def each(n, fn):
        def body(i, carry):
            fn(i)
            return carry
        lax.fori_loop(0, n, body, 0)

    def fill1(a):
        sb1[0, a] = total(xf * nc + a).astype(BF16)
        sb1[1, a] = total(xf * nc + hc + a).astype(BF16)
    each(hc, fill1)
    r1r = remote(sb1.at[0], rb1.at[0], r1_send.at[0], r1_recv.at[0], right)
    r1l = remote(sb1.at[1], rb1.at[1], r1_send.at[1], r1_recv.at[1], left)
    r1r.start()
    r1l.start()

    def part2(direction, h, n):
        s = sb2.at[direction, pl.ds(h * hc, hc)]
        d = rb2.at[direction, pl.ds(h * hc, hc)]
        return remote(s, d, r2_send.at[n], r2_recv.at[n], right if direction == 0 else left)

    def fill2(a):
        sb2[0, hc + a] = total(xr * nc + hc + a).astype(BF16)
        sb2[1, a] = total(xl * nc + a).astype(BF16)
    each(hc, fill2)
    m2 = [part2(0, 1, 0), part2(1, 0, 1), part2(0, 0, 2), part2(1, 1, 3)]
    m2[0].start()
    m2[1].start()
    r1r.wait_recv()

    def fill3(a):
        sb2[0, a] = (total(xr * nc + a) + rb1[0, a].astype(F32)).astype(BF16)
    each(hc, fill3)
    m2[2].start()
    r1l.wait_recv()

    def fill4(a):
        sb2[1, hc + a] = (total(xl * nc + hc + a) + rb1[1, a].astype(F32)).astype(BF16)
    each(hc, fill4)
    m2[3].start()
    for m in m2:
        m.wait_recv()

    def reduce(a):
        v = total(x * nc + a) + rb2[0, a].astype(F32) + rb2[1, a].astype(F32)
        red[a] = v
        zb[a] = v.astype(BF16)
    each(nc, reduce)
    ct = nc // NZ
    m3 = []
    for d in range(1, NZ):
        zz = lax.rem(z + d, NZ)
        m = remote(zb.at[pl.ds(zz * ct, ct)], zr.at[d - 1],
                   q_send.at[d - 1], q_recv.at[d - 1], (row, x * NZ + zz))
        m.start()
        m3.append(m)
    for m in m3:
        m.wait_recv()
    for b in range(ct):
        v = red[z * ct + b]
        for d in range(NZ - 1):
            v = v + zr[d, b].astype(F32)
        out_ref[b] = v.astype(BF16)

    for h in range(NZ):
        drain(h)
    to_up.wait_send()
    to_dn.wait_send()
    for m in [r1r, r1l] + m2 + m3:
        m.wait_send()


def shards(a_tiles, a_row, a_col, a_count, p_tiles):
    slots, width = a_tiles.shape[0], a_tiles.shape[1]
    pb = p_tiles.shape[0]
    n_row = lax.axis_size("row")
    n_col = lax.axis_size("col")
    nc = 3 * pb
    ct = nc * pb // n_col
    hc = nc // 2
    tile = (width, width)
    vm = pltpu.VMEM
    dma = pltpu.SemaphoreType.DMA
    smem = pl.BlockSpec(memory_space=pltpu.SMEM)
    vmem = pl.BlockSpec(memory_space=pltpu.VMEM)
    hbm = pl.BlockSpec(memory_space=pl.ANY)
    nj = 2 * NZ - 1
    return pl.pallas_call(
        functools.partial(kernel_body, n_row, pb, slots, width),
        out_shape=jax.ShapeDtypeStruct((ct,) + tile, BF16),
        in_specs=[smem, smem, smem, vmem, vmem, hbm, hbm],
        out_specs=vmem,
        scratch_shapes=[
            vm((slots,) + tile, BF16),
            vm((nc,) + tile, BF16),
            vm((n_col * pb,) + tile, BF16),
            vm((slots,) + tile, BF16),
            vm((slots,) + tile, F32),
            vm((8, slots), jnp.int32),
            pltpu.SMEM((8, slots), jnp.int32),
            vm((2, hc) + tile, BF16),
            vm((2, hc) + tile, BF16),
            vm((2, nc) + tile, BF16),
            vm((2, nc) + tile, BF16),
            vm((nc,) + tile, F32),
            vm((nc,) + tile, BF16),
            vm((NZ - 1, ct) + tile, BF16),
            dma((4,)), dma(()), dma(()), dma((2,)), dma((2,)),
            dma((2, NZ)), dma((2, NZ)),
            dma((2, nj)), dma((2, nj)), dma((2, nj)), dma((2, nj)),
            dma((2,)), dma((2,)), dma((4,)), dma((4,)), dma((NZ - 1,)), dma((NZ - 1,)),
        ],
        compiler_params=pltpu.CompilerParams(
            collective_id=0, has_side_effects=True, vmem_limit_bytes=48 << 20),
    )(a_col, a_row, a_count, a_col.reshape(1, slots), a_row.reshape(1, slots), a_tiles, p_tiles)


def solution(mesh):
    in_specs = (
        P(("row", "col"), None, None),
        P(("row", "col")),
        P(("row", "col")),
        P(("row", "col")),
        P(("row", "col"), None, None),
    )
    out_specs = P(("row", "col"), None, None)
    return jax.shard_map(shards, mesh=mesh, in_specs=in_specs, out_specs=out_specs, check_vma=False)
```

```python
import functools

import jax
import jax.numpy as jnp
from jax import lax
from jax.experimental import pallas as pl
from jax.experimental.pallas import tpu as pltpu
from jax.sharding import PartitionSpec as P

MESH = pl.DeviceIdType.MESH
F32 = jnp.float32
BF16 = jnp.bfloat16
I32 = jnp.int32
NX, NZ, NQ = 4, 6, 2


def kernel_body(
    n_row, pb, slots, width,
    acol_s, arow_s, acount_s, acol_v, arow_v, a_hbm, p_hbm, out_ref,
    abuf, colbuf, row0, row1, img, seg0, seg1, tabv, tabs,
    fbuf, frecv, nbuf, nrecv, red, zb, zr,
    a_sem, p_sem, t_sem, sh_send, sh_recv,
    z_send, z_recv, x_send, x_recv, y_send, y_recv,
    f_send, f_recv, n_send, n_recv, q_send, q_recv,
):
    row = lax.axis_index("row")
    col = lax.axis_index("col")
    x = col // NZ
    z = lax.rem(col, NZ)
    core = lax.rem(row, 2)
    late = lax.rem(row // 2, 2)
    nc = 3 * pb
    rows = width // NQ
    rowb = (row0, row1)
    segs = (seg0, seg1)
    mate = (row + 1 - 2 * core, col)
    far = (lax.rem(row + n_row - 1 + 2 * core, n_row), col)
    mate_at = core * (2 * pb)
    far_at = (1 - core) * (2 * pb)
    xr = lax.rem(x + 1, NX)
    xl = lax.rem(x + NX - 1, NX)
    xf = lax.rem(x + 2, NX)
    right = (row, xr * NZ + z)
    left = (row, xl * NZ + z)
    has_up = z < NZ - 1
    has_dn = z > 0
    zup = (row, x * NZ + lax.rem(z + 1, NZ))
    zdn = (row, x * NZ + lax.rem(z + NZ - 1, NZ))

    def remote(src, dst, ssem, rsem, dev):
        return pltpu.make_async_remote_copy(
            src_ref=src, dst_ref=dst, send_sem=ssem, recv_sem=rsem,
            device_id=dev, device_id_type=MESH)

    def signal(dev):
        pl.semaphore_signal(pltpu.get_barrier_semaphore(), inc=1, device_id=dev, device_id_type=MESH)

    own = colbuf.at[pl.ds(pb, pb)]
    p_copy = pltpu.make_async_copy(p_hbm, own, p_sem)
    p_copy.start()
    barrier = pltpu.get_barrier_semaphore()
    for dev in (right, left, mate):
        signal(dev)
    pl.when(has_up)(lambda: signal(zup))
    pl.when(has_dn)(lambda: signal(zdn))

    p_copy.wait()
    for k in range(pb):
        flipped = colbuf[pb + k].T
        for q in range(NQ):
            rowb[q][col * pb + k] = flipped[q * rows:(q + 1) * rows]

    near = 3 + has_up.astype(I32) + has_dn.astype(I32)
    pl.semaphore_wait(barrier, near + late)
    signal(far)

    half = pb // 2

    def z_msg(q, zz, dev):
        s = rowb[q].at[pl.ds((x * NZ + zz) * pb, pb)]
        return remote(s, s, z_send.at[q, zz], z_recv.at[q, zz], dev)

    def z_both(q, side):
        s = rowb[q].at[pl.ds(col * pb, pb)]
        return remote(s, s, z_send.at[q, NZ + side], z_recv.at[q, z], zup if side == 0 else zdn)

    def x_msg(q, d, xx, zz):
        s = rowb[q].at[pl.ds((xx * NZ + zz) * pb, pb)]
        return remote(s, s, x_send.at[q, d, zz], x_recv.at[q, d, zz], right if d == 0 else left)

    def y_msg(q, d, xx, zz):
        s = rowb[q].at[pl.ds((xx * NZ + zz) * pb + d * half, half)]
        return remote(s, s, y_send.at[q, d, zz], y_recv.at[q, d, zz], right if d == 0 else left)

    pairs = jnp.minimum(z, NZ - 1 - z)
    more_below = z > NZ - 1 - z

    def place(n):
        if n == 0:
            return z
        side = (z - (n + 1) // 2) if n % 2 else (z + n // 2)
        rest = jnp.where(more_below, z - (n - pairs), z + (n - pairs))
        return jnp.where(n <= 2 * pairs, side, rest)

    def step(q, n):
        if n == 0:
            pl.when(has_up)(lambda: z_both(q, 0).start())
            pl.when(has_dn)(lambda: z_both(q, 1).start())
            x_msg(q, 0, x, z).start()
            x_msg(q, 1, x, z).start()
            return
        zz = place(n)
        z_msg(q, zz, zup).wait_recv()
        pl.when((zz < z) & has_up)(lambda: z_msg(q, zz, zup).start())
        pl.when((zz > z) & has_dn)(lambda: z_msg(q, zz, zdn).start())
        x_msg(q, 0, x, zz).start()
        x_msg(q, 1, x, zz).start()

    def relay(q, n):
        zz = place(n)
        x_msg(q, 0, xl, zz).wait_recv()
        y_msg(q, 0, xl, zz).start()
        x_msg(q, 1, xr, zz).wait_recv()
        y_msg(q, 1, xr, zz).start()

    def arrived(q):
        for n in range(NZ):
            zz = place(n)
            y_msg(q, 0, xf, zz).wait_recv()
            y_msg(q, 1, xf, zz).wait_recv()

    def drain(q):
        pl.when(has_up)(lambda: z_both(q, 0).wait_send())
        pl.when(has_dn)(lambda: z_both(q, 1).wait_send())
        for n in range(NZ):
            zz = place(n)
            if n > 0:
                pl.when((zz < z) & has_up)(lambda: z_msg(q, zz, zup).wait_send())
                pl.when((zz > z) & has_dn)(lambda: z_msg(q, zz, zdn).wait_send())
            for d in range(2):
                x_msg(q, d, x, zz).wait_send()
                y_msg(q, d, x, zz).wait_send()

    step(0, 0)
    to_mate = remote(own, colbuf.at[pl.ds(mate_at, pb)], sh_send.at[0], sh_recv.at[0], mate)
    to_far = remote(own, colbuf.at[pl.ds(far_at, pb)], sh_send.at[1], sh_recv.at[1], far)
    to_mate.start()
    step(1, 0)
    pl.when(late == 1)(lambda: to_far.start())

    n_a = 4
    part = slots // n_a
    a_copies = [
        pltpu.make_async_copy(
            a_hbm.at[pl.ds(i * part, part)], abuf.at[pl.ds(i * part, part)], a_sem.at[i])
        for i in range(n_a)]
    for c in a_copies:
        c.start()

    lane = lax.broadcasted_iota(I32, (slots, slots), 1)
    sub = lax.broadcasted_iota(I32, (slots, slots), 0)
    acol = jnp.broadcast_to(acol_v[...], (slots, slots))
    arow = jnp.broadcast_to(arow_v[...], (slots, slots))
    n_out = nc * pb
    key = jnp.where(lane < acount_s[0], (arow & (pb - 1)) * nc + acol, n_out)
    key_t = key.T
    before = (key_t < key) | ((key_t == key) & (sub < lane))
    rank = jnp.sum(before.astype(I32), axis=0, keepdims=True)
    rank_t = jnp.broadcast_to(rank, (slots, slots)).T
    hit = rank_t == lane
    order = jnp.sum(jnp.where(hit, sub, 0), axis=0, keepdims=True)
    s_key = jnp.sum(jnp.where(hit, key_t, 0), axis=0, keepdims=True)
    last = jnp.sum((key_t <= lane).astype(I32), axis=0, keepdims=True) - 1
    some = jnp.sum((key_t == lane).astype(I32), axis=0, keepdims=True)
    s_key8 = jnp.broadcast_to(s_key, (8, slots))
    prev = pltpu.roll(s_key8, 1, 1)
    lane8 = lax.broadcasted_iota(I32, (8, slots), 1)
    keep = jnp.where((lane8 > 0) & (prev == s_key8), 1, 0)
    sub8 = lax.broadcasted_iota(I32, (8, slots), 0)
    tabv[...] = jnp.where(
        sub8 == 0, jnp.broadcast_to(order, (8, slots)),
        jnp.where(sub8 == 1, keep,
                  jnp.where(sub8 == 2, jnp.broadcast_to(jnp.maximum(last, 0), (8, slots)),
                            jnp.broadcast_to(jnp.minimum(some, 1), (8, slots)))))
    t_copy = pltpu.make_async_copy(tabv, tabs, t_sem)
    t_copy.start()

    U = 8

    def images(first, count):
        def body(i, carry):
            for u in range(U):
                t = first + i * U + u
                img[t] = jnp.dot(abuf[t], colbuf[acol_s[t]],
                                 preferred_element_type=F32).astype(BF16)
            return carry
        lax.fori_loop(0, count // U, body, 0)

    def terms(q, first, count):
        def body(i, carry):
            for u in range(U):
                p = first + i * U + u
                t = tabs[0, p]
                term = jnp.dot(rowb[q][arow_s[t]], img[t], preferred_element_type=F32)
                carry = carry * tabs[1, p].astype(F32) + term
                segs[q][p] = carry
            return carry
        start = jnp.zeros((rows, width), F32) if first == 0 else segs[q][first - 1]
        lax.fori_loop(0, count // U, body, start)

    ct = nc // NZ

    def total(q, s):
        return segs[q][tabs[2, s]] * tabs[3, s].astype(F32)

    def group(d, i):
        return i if d == 0 else NZ - 1 - i

    def far_msg(q, d, i):
        return remote(fbuf.at[q, d, i], frecv.at[q, d, i], f_send.at[q, d, i], f_recv.at[q, d, i],
                      right if d == 0 else left)

    def near_msg(q, d, g):
        return remote(nbuf.at[q, d, g], nrecv.at[q, d, g], n_send.at[q, d, g], n_recv.at[q, d, g],
                      right if d == 0 else left)

    def z_out(q, g):
        return remote(zb.at[q, g], zr.at[q, z], q_send.at[q, g], q_recv.at[q, z], (row, x * NZ + g))

    def send_far(q, i):
        for d in range(2):
            for b in range(ct):
                fbuf[q, d, i, b] = total(q, xf * nc + group(d, i) * ct + b).astype(BF16)
            far_msg(q, d, i).start()

    def send_near(q, i):
        for d in range(2):
            g = group(1 - d, i)
            for b in range(ct):
                nbuf[q, d, g, b] = total(q, (xr if d == 0 else xl) * nc + g * ct + b).astype(BF16)
            near_msg(q, d, g).start()

    def send_joint(q, i):
        for d in range(2):
            g = group(d, i)
            far_msg(q, d, i).wait_recv()
            for b in range(ct):
                v = total(q, (xr if d == 0 else xl) * nc + g * ct + b)
                nbuf[q, d, g, b] = (v + frecv[q, d, i, b].astype(F32)).astype(BF16)
            near_msg(q, d, g).start()

    def finish(q, i):
        for g in (group(0, i), group(1, i)):
            near_msg(q, 0, g).wait_recv()
            near_msg(q, 1, g).wait_recv()
            for b in range(ct):
                v = total(q, x * nc + g * ct + b)
                v = v + nrecv[q, 0, g, b].astype(F32) + nrecv[q, 1, g, b].astype(F32)
                zb[q, g, b] = v.astype(BF16)

                def keep_own(v=v, b=b):
                    red[q, b] = v
                pl.when(z == g)(keep_own)
            pl.when(z != g)(lambda g=g: z_out(q, g).start())

    def z_in(q, zz):
        return remote(zb.at[q, 0], zr.at[q, zz], q_send.at[q, 0], q_recv.at[q, zz], zup)

    def close(q):
        for d in range(1, NZ):
            z_in(q, lax.rem(z + d, NZ)).wait_recv()
        for b in range(ct):
            v = red[q, b]
            for d in range(1, NZ):
                v = v + zr[q, lax.rem(z + d, NZ), b].astype(F32)
            out_ref[b, pl.ds(q * rows, rows)] = v.astype(BF16)

    def far_start():
        pl.semaphore_wait(barrier, 1)
        to_far.start()

    for n in range(1, NZ):
        step(0, n)
        step(1, n)
        if n >= 2:
            relay(0, n - 2)
            relay(1, n - 2)
        if n == NZ - 2:
            pl.when(late == 0)(far_start)
    to_mate.wait_recv()
    to_far.wait_recv()
    for c in a_copies:
        c.wait()
    images(0, 64)
    relay(0, NZ - 2)
    relay(1, NZ - 2)
    images(64, 64)
    relay(0, NZ - 1)
    relay(1, NZ - 1)
    t_copy.wait()
    arrived(0)
    terms(0, 0, slots)
    send_far(0, 0)
    send_far(0, 1)
    send_near(0, 0)
    send_joint(0, 0)
    send_far(0, 2)
    send_near(0, 1)
    send_joint(0, 1)
    send_near(0, 2)
    arrived(1)
    terms(1, 0, 64)
    send_joint(0, 2)
    terms(1, 64, 64)
    send_far(1, 0)
    send_far(1, 1)
    send_near(1, 0)
    finish(0, 0)
    send_joint(1, 0)
    finish(0, 1)
    send_far(1, 2)
    send_near(1, 1)
    send_joint(1, 1)
    finish(0, 2)
    send_near(1, 2)
    send_joint(1, 2)
    finish(1, 0)
    finish(1, 1)
    finish(1, 2)
    close(0)
    close(1)

    to_mate.wait_send()
    to_far.wait_send()
    for q in range(NQ):
        drain(q)
        for d in range(2):
            for i in range(NZ // 2):
                far_msg(q, d, i).wait_send()
            for g in range(NZ):
                near_msg(q, d, g).wait_send()
        for g in range(NZ):
            pl.when(z != g)(lambda g=g: z_out(q, g).wait_send())


def shards(a_tiles, a_row, a_col, a_count, p_tiles):
    slots, width = a_tiles.shape[0], a_tiles.shape[1]
    pb = p_tiles.shape[0]
    n_row = lax.axis_size("row")
    n_col = lax.axis_size("col")
    nc = 3 * pb
    ct = nc * pb // n_col
    tile = (width, width)
    part = (width // NQ, width)
    vm = pltpu.VMEM
    dma = pltpu.SemaphoreType.DMA
    smem = pl.BlockSpec(memory_space=pltpu.SMEM)
    vmem = pl.BlockSpec(memory_space=pltpu.VMEM)
    hbm = pl.BlockSpec(memory_space=pl.ANY)
    ng = NZ // 2
    return pl.pallas_call(
        functools.partial(kernel_body, n_row, pb, slots, width),
        out_shape=jax.ShapeDtypeStruct((ct,) + tile, BF16),
        in_specs=[smem, smem, smem, vmem, vmem, hbm, hbm],
        out_specs=vmem,
        scratch_shapes=[
            vm((slots,) + tile, BF16),
            vm((nc,) + tile, BF16),
            vm((n_col * pb,) + part, BF16),
            vm((n_col * pb,) + part, BF16),
            vm((slots,) + tile, BF16),
            vm((slots,) + part, F32),
            vm((slots,) + part, F32),
            vm((8, slots), I32),
            pltpu.SMEM((8, slots), I32),
            vm((NQ, 2, ng, ct) + part, BF16),
            vm((NQ, 2, ng, ct) + part, BF16),
            vm((NQ, 2, NZ, ct) + part, BF16),
            vm((NQ, 2, NZ, ct) + part, BF16),
            vm((NQ, ct) + part, F32),
            vm((NQ, NZ, ct) + part, BF16),
            vm((NQ, NZ, ct) + part, BF16),
            dma((4,)), dma(()), dma(()), dma((2,)), dma((2,)),
            dma((NQ, NZ + 2)), dma((NQ, NZ)),
            dma((NQ, 2, NZ)), dma((NQ, 2, NZ)), dma((NQ, 2, NZ)), dma((NQ, 2, NZ)),
            dma((NQ, 2, ng)), dma((NQ, 2, ng)), dma((NQ, 2, NZ)), dma((NQ, 2, NZ)),
            dma((NQ, NZ)), dma((NQ, NZ)),
        ],
        compiler_params=pltpu.CompilerParams(
            collective_id=0, has_side_effects=True, vmem_limit_bytes=67043328),
    )(a_col, a_row, a_count, a_col.reshape(1, slots), a_row.reshape(1, slots), a_tiles, p_tiles)


def solution(mesh):
    in_specs = (
        P(("row", "col"), None, None),
        P(("row", "col")),
        P(("row", "col")),
        P(("row", "col")),
        P(("row", "col"), None, None),
    )
    out_specs = P(("row", "col"), None, None)
    return jax.shard_map(shards, mesh=mesh, in_specs=in_specs, out_specs=out_specs, check_vma=False)
```

```python
import functools

import jax
import jax.numpy as jnp
from jax import lax
from jax.experimental import pallas as pl
from jax.experimental.pallas import tpu as pltpu
from jax.sharding import PartitionSpec as P

MESH = pl.DeviceIdType.MESH
F32 = jnp.float32
BF16 = jnp.bfloat16
I32 = jnp.int32
NX, NZ, NQ = 4, 6, 2


def kernel_body(
    n_row, pb, slots, width,
    acol_h, arow_h, acount_h, a_hbm, p_hbm, out_ref,
    abuf, colbuf, row0, row1, img, seg0, seg1, tabv, tabs,
    fbuf, frecv, nbuf, nrecv, red, zb, zr,
    acol_s, arow_s, acount_s, acol_v, arow_v, s_sem,
    a_sem, p_sem, t_sem, sh_send, sh_recv,
    z_send, z_recv, x_send, x_recv, y_send, y_recv,
    f_send, f_recv, n_send, n_recv, q_send, q_recv,
):
    row = lax.axis_index("row")
    col = lax.axis_index("col")
    x = col // NZ
    z = lax.rem(col, NZ)
    core = lax.rem(row, 2)
    late = lax.rem(row // 2, 2)
    nc = 3 * pb
    rows = width // NQ
    rowb = (row0, row1)
    segs = (seg0, seg1)
    mate = (row + 1 - 2 * core, col)
    far = (lax.rem(row + n_row - 1 + 2 * core, n_row), col)
    mate_at = core * (2 * pb)
    far_at = (1 - core) * (2 * pb)
    xr = lax.rem(x + 1, NX)
    xl = lax.rem(x + NX - 1, NX)
    xf = lax.rem(x + 2, NX)
    right = (row, xr * NZ + z)
    left = (row, xl * NZ + z)
    has_up = z < NZ - 1
    has_dn = z > 0
    zup = (row, x * NZ + lax.rem(z + 1, NZ))
    zdn = (row, x * NZ + lax.rem(z + NZ - 1, NZ))

    def remote(src, dst, ssem, rsem, dev):
        return pltpu.make_async_remote_copy(
            src_ref=src, dst_ref=dst, send_sem=ssem, recv_sem=rsem,
            device_id=dev, device_id_type=MESH)

    def signal(dev):
        pl.semaphore_signal(pltpu.get_barrier_semaphore(), inc=1, device_id=dev, device_id_type=MESH)

    own = colbuf.at[pl.ds(pb, pb)]
    p_copy = pltpu.make_async_copy(p_hbm, own, p_sem)
    p_copy.start()
    small = [
        pltpu.make_async_copy(src, dst, s_sem.at[i]) for i, (src, dst) in enumerate((
            (acol_h, acol_s), (arow_h, arow_s), (acount_h, acount_s),
            (acol_h, acol_v), (arow_h, arow_v)))]
    barrier = pltpu.get_barrier_semaphore()
    for dev in (right, left, mate):
        signal(dev)
    pl.when(has_up)(lambda: signal(zup))
    pl.when(has_dn)(lambda: signal(zdn))

    p_copy.wait()
    for k in range(pb):
        flipped = colbuf[pb + k].T
        for q in range(NQ):
            rowb[q][col * pb + k] = flipped[q * rows:(q + 1) * rows]

    near = 3 + has_up.astype(I32) + has_dn.astype(I32)
    pl.semaphore_wait(barrier, near + late)
    signal(far)

    half = pb // 2

    def z_msg(q, zz, h, dev):
        s = rowb[q].at[pl.ds((x * NZ + zz) * pb + h * half, half)]
        return remote(s, s, z_send.at[q, h, zz], z_recv.at[q, h, zz], dev)

    def z_both(q, side, h):
        s = rowb[q].at[pl.ds(col * pb + h * half, half)]
        return remote(s, s, z_send.at[q, h, NZ + side], z_recv.at[q, h, z], zup if side == 0 else zdn)

    def x_msg(q, d, xx, zz):
        s = rowb[q].at[pl.ds((xx * NZ + zz) * pb, pb)]
        return remote(s, s, x_send.at[q, d, zz], x_recv.at[q, d, zz], right if d == 0 else left)

    def y_msg(q, d, xx, zz):
        s = rowb[q].at[pl.ds((xx * NZ + zz) * pb + d * half, half)]
        return remote(s, s, y_send.at[q, d, zz], y_recv.at[q, d, zz], right if d == 0 else left)

    pairs = jnp.minimum(z, NZ - 1 - z)
    more_below = z > NZ - 1 - z

    def place(n):
        if n == 0:
            return z
        side = (z - (n + 1) // 2) if n % 2 else (z + n // 2)
        rest = jnp.where(more_below, z - (n - pairs), z + (n - pairs))
        return jnp.where(n <= 2 * pairs, side, rest)

    def step(q, n):
        zz = place(n)
        for h in range(2):
            if n == 0:
                pl.when(has_up)(lambda h=h: z_both(q, 0, h).start())
                pl.when(has_dn)(lambda h=h: z_both(q, 1, h).start())
            else:
                z_msg(q, zz, h, zup).wait_recv()
                pl.when((zz < z) & has_up)(lambda h=h: z_msg(q, zz, h, zup).start())
                pl.when((zz > z) & has_dn)(lambda h=h: z_msg(q, zz, h, zdn).start())
        x_msg(q, 0, x, zz).start()
        x_msg(q, 1, x, zz).start()

    def relay(q, n):
        zz = place(n)
        x_msg(q, 0, xl, zz).wait_recv()
        y_msg(q, 0, xl, zz).start()
        x_msg(q, 1, xr, zz).wait_recv()
        y_msg(q, 1, xr, zz).start()

    def arrived(q):
        for n in range(NZ):
            zz = place(n)
            y_msg(q, 0, xf, zz).wait_recv()
            y_msg(q, 1, xf, zz).wait_recv()

    def drain(q):
        for h in range(2):
            pl.when(has_up)(lambda h=h: z_both(q, 0, h).wait_send())
            pl.when(has_dn)(lambda h=h: z_both(q, 1, h).wait_send())
        for n in range(NZ):
            zz = place(n)
            for h in range(2 if n > 0 else 0):
                pl.when((zz < z) & has_up)(lambda h=h, zz=zz: z_msg(q, zz, h, zup).wait_send())
                pl.when((zz > z) & has_dn)(lambda h=h, zz=zz: z_msg(q, zz, h, zdn).wait_send())
            for d in range(2):
                x_msg(q, d, x, zz).wait_send()
                y_msg(q, d, x, zz).wait_send()

    step(0, 0)
    to_mate = remote(own, colbuf.at[pl.ds(mate_at, pb)], sh_send.at[0], sh_recv.at[0], mate)
    to_far = remote(own, colbuf.at[pl.ds(far_at, pb)], sh_send.at[1], sh_recv.at[1], far)
    to_mate.start()
    step(1, 0)
    pl.when(late == 1)(lambda: to_far.start())

    n_a = 4
    part = slots // n_a
    a_copies = [
        pltpu.make_async_copy(
            a_hbm.at[pl.ds(i * part, part)], abuf.at[pl.ds(i * part, part)], a_sem.at[i])
        for i in range(n_a)]
    for c in small + a_copies:
        c.start()

    for c in small:
        c.wait()
    lane = lax.broadcasted_iota(I32, (slots, slots), 1)
    sub = lax.broadcasted_iota(I32, (slots, slots), 0)
    acol = jnp.broadcast_to(acol_v[...].reshape(1, slots), (slots, slots))
    arow = jnp.broadcast_to(arow_v[...].reshape(1, slots), (slots, slots))
    n_out = nc * pb
    key = jnp.where(lane < acount_s[0], (arow & (pb - 1)) * nc + acol, n_out)
    key_t = key.T
    before = (key_t < key) | ((key_t == key) & (sub < lane))
    rank = jnp.sum(before.astype(I32), axis=0, keepdims=True)
    rank_t = jnp.broadcast_to(rank, (slots, slots)).T
    hit = rank_t == lane
    order = jnp.sum(jnp.where(hit, sub, 0), axis=0, keepdims=True)
    s_key = jnp.sum(jnp.where(hit, key_t, 0), axis=0, keepdims=True)
    last = jnp.sum((key_t <= lane).astype(I32), axis=0, keepdims=True) - 1
    some = jnp.sum((key_t == lane).astype(I32), axis=0, keepdims=True)
    s_key8 = jnp.broadcast_to(s_key, (8, slots))
    prev = pltpu.roll(s_key8, 1, 1)
    lane8 = lax.broadcasted_iota(I32, (8, slots), 1)
    keep = jnp.where((lane8 > 0) & (prev == s_key8), 1, 0)
    sub8 = lax.broadcasted_iota(I32, (8, slots), 0)
    tabv[...] = jnp.where(
        sub8 == 0, jnp.broadcast_to(order, (8, slots)),
        jnp.where(sub8 == 1, keep,
                  jnp.where(sub8 == 2, jnp.broadcast_to(jnp.maximum(last, 0), (8, slots)),
                            jnp.broadcast_to(jnp.minimum(some, 1), (8, slots)))))
    t_copy = pltpu.make_async_copy(tabv, tabs, t_sem)
    t_copy.start()

    U = 8

    def images(first, count):
        def body(i, carry):
            for u in range(U):
                t = first + i * U + u
                img[t] = jnp.dot(abuf[t], colbuf[acol_s[t]],
                                 preferred_element_type=F32).astype(BF16)
            return carry
        lax.fori_loop(0, count // U, body, 0)

    def terms(q, first, count):
        def body(i, carry):
            for u in range(U):
                p = first + i * U + u
                t = tabs[0, p]
                term = jnp.dot(rowb[q][arow_s[t]], img[t], preferred_element_type=F32)
                carry = carry * tabs[1, p].astype(F32) + term
                segs[q][p] = carry
            return carry
        start = jnp.zeros((rows, width), F32) if first == 0 else segs[q][first - 1]
        lax.fori_loop(0, count // U, body, start)

    ct = nc // NZ

    def total(q, s):
        return segs[q][tabs[2, s]] * tabs[3, s].astype(F32)

    def group(d, i):
        return i if d == 0 else NZ - 1 - i

    def far_msg(q, d, i):
        return remote(fbuf.at[q, d, i], frecv.at[q, d, i], f_send.at[q, d, i], f_recv.at[q, d, i],
                      right if d == 0 else left)

    def near_msg(q, d, g):
        return remote(nbuf.at[q, d, g], nrecv.at[q, d, g], n_send.at[q, d, g], n_recv.at[q, d, g],
                      right if d == 0 else left)

    def z_out(q, g):
        return remote(zb.at[q, g], zr.at[q, z], q_send.at[q, g], q_recv.at[q, z], (row, x * NZ + g))

    def send_far(q, i):
        for d in range(2):
            for b in range(ct):
                fbuf[q, d, i, b] = total(q, xf * nc + group(d, i) * ct + b).astype(BF16)
            far_msg(q, d, i).start()

    def send_near(q, i):
        for d in range(2):
            g = group(1 - d, i)
            for b in range(ct):
                nbuf[q, d, g, b] = total(q, (xr if d == 0 else xl) * nc + g * ct + b).astype(BF16)
            near_msg(q, d, g).start()

    def send_joint(q, i):
        for d in range(2):
            g = group(d, i)
            far_msg(q, d, i).wait_recv()
            for b in range(ct):
                v = total(q, (xr if d == 0 else xl) * nc + g * ct + b)
                nbuf[q, d, g, b] = (v + frecv[q, d, i, b].astype(F32)).astype(BF16)
            near_msg(q, d, g).start()

    def finish(q, i):
        for g in (group(0, i), group(1, i)):
            near_msg(q, 0, g).wait_recv()
            near_msg(q, 1, g).wait_recv()
            for b in range(ct):
                v = total(q, x * nc + g * ct + b)
                v = v + nrecv[q, 0, g, b].astype(F32) + nrecv[q, 1, g, b].astype(F32)
                zb[q, g, b] = v.astype(BF16)

                def keep_own(v=v, b=b):
                    red[q, b] = v
                pl.when(z == g)(keep_own)
            pl.when(z != g)(lambda g=g: z_out(q, g).start())

    def z_in(q, zz):
        return remote(zb.at[q, 0], zr.at[q, zz], q_send.at[q, 0], q_recv.at[q, zz], zup)

    def close(q):
        for d in range(1, NZ):
            z_in(q, lax.rem(z + d, NZ)).wait_recv()
        for b in range(ct):
            v = red[q, b]
            for d in range(1, NZ):
                v = v + zr[q, lax.rem(z + d, NZ), b].astype(F32)
            out_ref[b, pl.ds(q * rows, rows)] = v.astype(BF16)

    def far_start():
        pl.semaphore_wait(barrier, 1)
        to_far.start()

    for n in range(1, NZ):
        step(0, n)
        step(1, n)
        if n >= 2:
            relay(0, n - 2)
            relay(1, n - 2)
        if n == NZ - 2:
            pl.when(late == 0)(far_start)
    to_mate.wait_recv()
    to_far.wait_recv()
    for c in a_copies:
        c.wait()
    quarter = slots // 4
    for i, (n, q) in enumerate([(NZ - 2, 0), (NZ - 2, 1), (NZ - 1, 0), (NZ - 1, 1)]):
        images(i * quarter, quarter)
        relay(q, n)
    t_copy.wait()
    arrived(0)
    terms(0, 0, slots)
    arrived(1)
    for i in range(NZ // 2):
        send_far(0, i)
    for i in range(NZ // 2):
        send_near(0, i)
    terms(1, 0, slots // 2)
    for i in range(NZ // 2):
        send_joint(0, i)
    terms(1, slots // 2, slots // 2)
    for i in range(NZ // 2):
        send_far(1, i)
    for i in range(NZ // 2):
        send_near(1, i)
    for i in range(NZ // 2):
        finish(0, i)
    for i in range(NZ // 2):
        send_joint(1, i)
    close(0)
    for i in range(NZ // 2):
        finish(1, i)
    close(1)

    to_mate.wait_send()
    to_far.wait_send()
    for q in range(NQ):
        drain(q)
        for d in range(2):
            for i in range(NZ // 2):
                far_msg(q, d, i).wait_send()
            for g in range(NZ):
                near_msg(q, d, g).wait_send()
        for g in range(NZ):
            pl.when(z != g)(lambda g=g: z_out(q, g).wait_send())


def shards(a_tiles, a_row, a_col, a_count, p_tiles):
    slots, width = a_tiles.shape[0], a_tiles.shape[1]
    pb = p_tiles.shape[0]
    n_row = lax.axis_size("row")
    n_col = lax.axis_size("col")
    nc = 3 * pb
    ct = nc * pb // n_col
    tile = (width, width)
    part = (width // NQ, width)
    vm = pltpu.VMEM
    dma = pltpu.SemaphoreType.DMA
    vmem = pl.BlockSpec(memory_space=pltpu.VMEM)
    hbm = pl.BlockSpec(memory_space=pltpu.HBM)
    ng = NZ // 2
    return pl.pallas_call(
        functools.partial(kernel_body, n_row, pb, slots, width),
        out_shape=jax.ShapeDtypeStruct((ct,) + tile, BF16),
        in_specs=[hbm] * 5,
        out_specs=vmem,
        scratch_shapes=[
            vm((slots,) + tile, BF16),
            vm((nc,) + tile, BF16),
            vm((n_col * pb,) + part, BF16),
            vm((n_col * pb,) + part, BF16),
            vm((slots,) + tile, BF16),
            vm((slots,) + part, F32),
            vm((slots,) + part, F32),
            vm((8, slots), I32),
            pltpu.SMEM((8, slots), I32),
            vm((NQ, 2, ng, ct) + part, BF16),
            vm((NQ, 2, ng, ct) + part, BF16),
            vm((NQ, 2, NZ, ct) + part, BF16),
            vm((NQ, 2, NZ, ct) + part, BF16),
            vm((NQ, ct) + part, F32),
            vm((NQ, NZ, ct) + part, BF16),
            vm((NQ, NZ, ct) + part, BF16),
            pltpu.SMEM((slots,), I32), pltpu.SMEM((slots,), I32), pltpu.SMEM((1,), I32),
            vm((slots,), I32), vm((slots,), I32), dma((5,)),
            dma((4,)), dma(()), dma(()), dma((2,)), dma((2,)),
            dma((NQ, 2, NZ + 2)), dma((NQ, 2, NZ)),
            dma((NQ, 2, NZ)), dma((NQ, 2, NZ)), dma((NQ, 2, NZ)), dma((NQ, 2, NZ)),
            dma((NQ, 2, ng)), dma((NQ, 2, ng)), dma((NQ, 2, NZ)), dma((NQ, 2, NZ)),
            dma((NQ, NZ)), dma((NQ, NZ)),
        ],
        compiler_params=pltpu.CompilerParams(
            collective_id=0, has_side_effects=True, vmem_limit_bytes=67043328),
    )(a_col, a_row, a_count, a_tiles, p_tiles)


def solution(mesh):
    in_specs = (
        P(("row", "col"), None, None),
        P(("row", "col")),
        P(("row", "col")),
        P(("row", "col")),
        P(("row", "col"), None, None),
    )
    out_specs = P(("row", "col"), None, None)
    return jax.shard_map(shards, mesh=mesh, in_specs=in_specs, out_specs=out_specs, check_vma=False)
```

```python
import functools

import jax
import jax.numpy as jnp
from jax import lax
from jax.experimental import pallas as pl
from jax.experimental.pallas import tpu as pltpu
from jax.sharding import PartitionSpec as P

MESH = pl.DeviceIdType.MESH
F32 = jnp.float32
BF16 = jnp.bfloat16
I32 = jnp.int32
NX, NZ, NQ = 4, 6, 2


def kernel_body(
    n_row, pb, slots, width,
    acol_h, arow_h, acount_h, a_hbm, p_hbm, out_ref,
    abuf, colbuf, row0, row1, img, seg0, seg1, tabv, tabs,
    fbuf, frecv, nbuf, nrecv, red, zb, zr,
    acol_s, arow_s, acount_s, acol_v, arow_v, s_sem,
    a_sem, p_sem, t_sem, sh_send, sh_recv,
    z_send, z_recv, x_send, x_recv, y_send, y_recv,
    f_send, f_recv, n_send, n_recv, q_send, q_recv,
):
    row = lax.axis_index("row")
    col = lax.axis_index("col")
    x = col // NZ
    z = lax.rem(col, NZ)
    core = lax.rem(row, 2)
    late = lax.rem(row // 2, 2)
    nc = 3 * pb
    rows = width // NQ
    rowb = (row0, row1)
    segs = (seg0, seg1)
    mate = (row + 1 - 2 * core, col)
    far = (lax.rem(row + n_row - 1 + 2 * core, n_row), col)
    mate_at = core * (2 * pb)
    far_at = (1 - core) * (2 * pb)
    xr = lax.rem(x + 1, NX)
    xl = lax.rem(x + NX - 1, NX)
    xf = lax.rem(x + 2, NX)
    right = (row, xr * NZ + z)
    left = (row, xl * NZ + z)
    has_up = z < NZ - 1
    has_dn = z > 0
    zup = (row, x * NZ + lax.rem(z + 1, NZ))
    zdn = (row, x * NZ + lax.rem(z + NZ - 1, NZ))

    def remote(src, dst, ssem, rsem, dev):
        return pltpu.make_async_remote_copy(
            src_ref=src, dst_ref=dst, send_sem=ssem, recv_sem=rsem,
            device_id=dev, device_id_type=MESH)

    def signal(dev):
        pl.semaphore_signal(pltpu.get_barrier_semaphore(), inc=1, device_id=dev, device_id_type=MESH)

    own = colbuf.at[pl.ds(pb, pb)]
    p_copy = pltpu.make_async_copy(p_hbm, own, p_sem)
    p_copy.start()
    small = [
        pltpu.make_async_copy(src, dst, s_sem.at[i]) for i, (src, dst) in enumerate((
            (acol_h, acol_s), (arow_h, arow_s), (acount_h, acount_s),
            (acol_h, acol_v), (arow_h, arow_v)))]
    barrier = pltpu.get_barrier_semaphore()
    for dev in (right, left, mate):
        signal(dev)
    pl.when(has_up)(lambda: signal(zup))
    pl.when(has_dn)(lambda: signal(zdn))

    p_copy.wait()
    for k in range(pb):
        flipped = colbuf[pb + k].T
        for q in range(NQ):
            rowb[q][col * pb + k] = flipped[q * rows:(q + 1) * rows]

    near = 3 + has_up.astype(I32) + has_dn.astype(I32)
    pl.semaphore_wait(barrier, near + late)
    signal(far)

    half = pb // 2

    def z_msg(q, zz, h, dev):
        s = rowb[q].at[pl.ds((x * NZ + zz) * pb + h * half, half)]
        return remote(s, s, z_send.at[q, h, zz], z_recv.at[q, h, zz], dev)

    def z_both(q, side, h):
        s = rowb[q].at[pl.ds(col * pb + h * half, half)]
        return remote(s, s, z_send.at[q, h, NZ + side], z_recv.at[q, h, z], zup if side == 0 else zdn)

    def x_msg(q, d, xx, zz):
        s = rowb[q].at[pl.ds((xx * NZ + zz) * pb, pb)]
        return remote(s, s, x_send.at[q, d, zz], x_recv.at[q, d, zz], right if d == 0 else left)

    def y_msg(q, d, xx, zz):
        s = rowb[q].at[pl.ds((xx * NZ + zz) * pb + d * half, half)]
        return remote(s, s, y_send.at[q, d, zz], y_recv.at[q, d, zz], right if d == 0 else left)

    pairs = jnp.minimum(z, NZ - 1 - z)
    more_below = z > NZ - 1 - z

    def place(n):
        if n == 0:
            return z
        side = (z - (n + 1) // 2) if n % 2 else (z + n // 2)
        rest = jnp.where(more_below, z - (n - pairs), z + (n - pairs))
        return jnp.where(n <= 2 * pairs, side, rest)

    def step(q, n):
        zz = place(n)
        for h in range(2):
            if n == 0:
                pl.when(has_up)(lambda h=h: z_both(q, 0, h).start())
                pl.when(has_dn)(lambda h=h: z_both(q, 1, h).start())
            else:
                z_msg(q, zz, h, zup).wait_recv()
                pl.when((zz < z) & has_up)(lambda h=h: z_msg(q, zz, h, zup).start())
                pl.when((zz > z) & has_dn)(lambda h=h: z_msg(q, zz, h, zdn).start())
        x_msg(q, 0, x, zz).start()
        x_msg(q, 1, x, zz).start()

    def relay(q, n):
        zz = place(n)
        x_msg(q, 0, xl, zz).wait_recv()
        y_msg(q, 0, xl, zz).start()
        x_msg(q, 1, xr, zz).wait_recv()
        y_msg(q, 1, xr, zz).start()

    def arrived(q):
        for n in range(NZ):
            zz = place(n)
            y_msg(q, 0, xf, zz).wait_recv()
            y_msg(q, 1, xf, zz).wait_recv()

    def drain(q):
        for h in range(2):
            pl.when(has_up)(lambda h=h: z_both(q, 0, h).wait_send())
            pl.when(has_dn)(lambda h=h: z_both(q, 1, h).wait_send())
        for n in range(NZ):
            zz = place(n)
            for h in range(2 if n > 0 else 0):
                pl.when((zz < z) & has_up)(lambda h=h, zz=zz: z_msg(q, zz, h, zup).wait_send())
                pl.when((zz > z) & has_dn)(lambda h=h, zz=zz: z_msg(q, zz, h, zdn).wait_send())
            for d in range(2):
                x_msg(q, d, x, zz).wait_send()
                y_msg(q, d, x, zz).wait_send()

    step(0, 0)
    to_mate = remote(own, colbuf.at[pl.ds(mate_at, pb)], sh_send.at[0], sh_recv.at[0], mate)
    to_far = remote(own, colbuf.at[pl.ds(far_at, pb)], sh_send.at[1], sh_recv.at[1], far)
    to_mate.start()
    step(1, 0)
    pl.when(late == 1)(lambda: to_far.start())

    n_a = 4
    part = slots // n_a
    a_copies = [
        pltpu.make_async_copy(
            a_hbm.at[pl.ds(i * part, part)], abuf.at[pl.ds(i * part, part)], a_sem.at[i])
        for i in range(n_a)]
    for c in small + a_copies:
        c.start()

    for c in small:
        c.wait()
    lane = lax.broadcasted_iota(I32, (slots, slots), 1)
    sub = lax.broadcasted_iota(I32, (slots, slots), 0)
    acol = jnp.broadcast_to(acol_v[...].reshape(1, slots), (slots, slots))
    arow = jnp.broadcast_to(arow_v[...].reshape(1, slots), (slots, slots))
    n_out = nc * pb
    key = jnp.where(lane < acount_s[0], (arow & (pb - 1)) * nc + acol, n_out)
    key_t = key.T
    before = (key_t < key) | ((key_t == key) & (sub < lane))
    rank = jnp.sum(before.astype(I32), axis=0, keepdims=True)
    rank_t = jnp.broadcast_to(rank, (slots, slots)).T
    hit = rank_t == lane
    order = jnp.sum(jnp.where(hit, sub, 0), axis=0, keepdims=True)
    s_key = jnp.sum(jnp.where(hit, key_t, 0), axis=0, keepdims=True)
    last = jnp.sum((key_t <= lane).astype(I32), axis=0, keepdims=True) - 1
    some = jnp.sum((key_t == lane).astype(I32), axis=0, keepdims=True)
    s_key8 = jnp.broadcast_to(s_key, (8, slots))
    prev = pltpu.roll(s_key8, 1, 1)
    lane8 = lax.broadcasted_iota(I32, (8, slots), 1)
    keep = jnp.where((lane8 > 0) & (prev == s_key8), 1, 0)
    sub8 = lax.broadcasted_iota(I32, (8, slots), 0)
    tabv[...] = jnp.where(
        sub8 == 0, jnp.broadcast_to(order, (8, slots)),
        jnp.where(sub8 == 1, keep,
                  jnp.where(sub8 == 2, jnp.broadcast_to(jnp.maximum(last, 0), (8, slots)),
                            jnp.broadcast_to(jnp.minimum(some, 1), (8, slots)))))
    t_copy = pltpu.make_async_copy(tabv, tabs, t_sem)
    t_copy.start()

    U = 32

    def images(first, count):
        def body(i, carry):
            for u in range(U):
                t = first + i * U + u
                img[t] = jnp.dot(abuf[t], colbuf[acol_s[t]],
                                 preferred_element_type=F32).astype(BF16)
            return carry
        lax.fori_loop(0, count // U, body, 0)

    def terms(q, first, count):
        def body(i, carry):
            for u in range(U):
                p = first + i * U + u
                t = tabs[0, p]
                term = jnp.dot(rowb[q][arow_s[t]], img[t], preferred_element_type=F32)
                carry = carry * tabs[1, p].astype(F32) + term
                segs[q][p] = carry
            return carry
        start = jnp.zeros((rows, width), F32) if first == 0 else segs[q][first - 1]
        lax.fori_loop(0, count // U, body, start)

    ct = nc // NZ

    def total(q, s):
        return segs[q][tabs[2, s]] * tabs[3, s].astype(F32)

    def group(d, i):
        return i if d == 0 else NZ - 1 - i

    def far_msg(q, d, i):
        return remote(fbuf.at[q, d, i], frecv.at[q, d, i], f_send.at[q, d, i], f_recv.at[q, d, i],
                      right if d == 0 else left)

    def near_msg(q, d, g):
        return remote(nbuf.at[q, d, g], nrecv.at[q, d, g], n_send.at[q, d, g], n_recv.at[q, d, g],
                      right if d == 0 else left)

    def z_out(q, g):
        return remote(zb.at[q, g], zr.at[q, z], q_send.at[q, g], q_recv.at[q, z], (row, x * NZ + g))

    def send_far(q, i):
        for d in range(2):
            for b in range(ct):
                fbuf[q, d, i, b] = total(q, xf * nc + group(d, i) * ct + b).astype(BF16)
            far_msg(q, d, i).start()

    def send_near(q, i):
        for d in range(2):
            g = group(1 - d, i)
            for b in range(ct):
                nbuf[q, d, g, b] = total(q, (xr if d == 0 else xl) * nc + g * ct + b).astype(BF16)
            near_msg(q, d, g).start()

    def send_joint(q, i):
        for d in range(2):
            g = group(d, i)
            far_msg(q, d, i).wait_recv()
            for b in range(ct):
                v = total(q, (xr if d == 0 else xl) * nc + g * ct + b)
                nbuf[q, d, g, b] = (v + frecv[q, d, i, b].astype(F32)).astype(BF16)
            near_msg(q, d, g).start()

    def finish(q, i):
        for g in (group(0, i), group(1, i)):
            near_msg(q, 0, g).wait_recv()
            near_msg(q, 1, g).wait_recv()
            for b in range(ct):
                v = total(q, x * nc + g * ct + b)
                v = v + nrecv[q, 0, g, b].astype(F32) + nrecv[q, 1, g, b].astype(F32)
                zb[q, g, b] = v.astype(BF16)

                def keep_own(v=v, b=b):
                    red[q, b] = v
                pl.when(z == g)(keep_own)
            pl.when(z != g)(lambda g=g: z_out(q, g).start())

    def z_in(q, zz):
        return remote(zb.at[q, 0], zr.at[q, zz], q_send.at[q, 0], q_recv.at[q, zz], zup)

    def close(q):
        for d in range(1, NZ):
            z_in(q, lax.rem(z + d, NZ)).wait_recv()
        for b in range(ct):
            v = red[q, b]
            for d in range(1, NZ):
                v = v + zr[q, lax.rem(z + d, NZ), b].astype(F32)
            out_ref[b, pl.ds(q * rows, rows)] = v.astype(BF16)

    def far_start():
        pl.semaphore_wait(barrier, 1)
        to_far.start()

    for n in range(1, NZ):
        step(0, n)
        step(1, n)
        if n >= 2:
            relay(0, n - 2)
            relay(1, n - 2)
        if n == NZ - 2:
            pl.when(late == 0)(far_start)
    to_mate.wait_recv()
    to_far.wait_recv()
    for c in a_copies:
        c.wait()
    quarter = slots // 4
    for i, (n, q) in enumerate([(NZ - 2, 0), (NZ - 2, 1), (NZ - 1, 0), (NZ - 1, 1)]):
        images(i * quarter, quarter)
        relay(q, n)
    t_copy.wait()
    arrived(0)
    terms(0, 0, slots)
    arrived(1)
    for i in range(NZ // 2):
        send_far(0, i)
    for i in range(NZ // 2):
        send_near(0, i)
    terms(1, 0, slots // 2)
    for i in range(NZ // 2):
        send_joint(0, i)
    terms(1, slots // 2, slots // 2)
    for i in range(NZ // 2):
        send_far(1, i)
    for i in range(NZ // 2):
        send_near(1, i)
    for i in range(NZ // 2):
        finish(0, i)
    for i in range(NZ // 2):
        send_joint(1, i)
    close(0)
    for i in range(NZ // 2):
        finish(1, i)
    close(1)

    to_mate.wait_send()
    to_far.wait_send()
    for q in range(NQ):
        drain(q)
        for d in range(2):
            for i in range(NZ // 2):
                far_msg(q, d, i).wait_send()
            for g in range(NZ):
                near_msg(q, d, g).wait_send()
        for g in range(NZ):
            pl.when(z != g)(lambda g=g: z_out(q, g).wait_send())


def shards(a_tiles, a_row, a_col, a_count, p_tiles):
    slots, width = a_tiles.shape[0], a_tiles.shape[1]
    pb = p_tiles.shape[0]
    n_row = lax.axis_size("row")
    n_col = lax.axis_size("col")
    nc = 3 * pb
    ct = nc * pb // n_col
    tile = (width, width)
    part = (width // NQ, width)
    vm = pltpu.VMEM
    dma = pltpu.SemaphoreType.DMA
    vmem = pl.BlockSpec(memory_space=pltpu.VMEM)
    hbm = pl.BlockSpec(memory_space=pltpu.HBM)
    ng = NZ // 2
    return pl.pallas_call(
        functools.partial(kernel_body, n_row, pb, slots, width),
        out_shape=jax.ShapeDtypeStruct((ct,) + tile, BF16),
        in_specs=[hbm] * 5,
        out_specs=vmem,
        scratch_shapes=[
            vm((slots,) + tile, BF16),
            vm((nc,) + tile, BF16),
            vm((n_col * pb,) + part, BF16),
            vm((n_col * pb,) + part, BF16),
            vm((slots,) + tile, BF16),
            vm((slots,) + part, F32),
            vm((slots,) + part, F32),
            vm((8, slots), I32),
            pltpu.SMEM((8, slots), I32),
            vm((NQ, 2, ng, ct) + part, BF16),
            vm((NQ, 2, ng, ct) + part, BF16),
            vm((NQ, 2, NZ, ct) + part, BF16),
            vm((NQ, 2, NZ, ct) + part, BF16),
            vm((NQ, ct) + part, F32),
            vm((NQ, NZ, ct) + part, BF16),
            vm((NQ, NZ, ct) + part, BF16),
            pltpu.SMEM((slots,), I32), pltpu.SMEM((slots,), I32), pltpu.SMEM((1,), I32),
            vm((slots,), I32), vm((slots,), I32), dma((5,)),
            dma((4,)), dma(()), dma(()), dma((2,)), dma((2,)),
            dma((NQ, 2, NZ + 2)), dma((NQ, 2, NZ)),
            dma((NQ, 2, NZ)), dma((NQ, 2, NZ)), dma((NQ, 2, NZ)), dma((NQ, 2, NZ)),
            dma((NQ, 2, ng)), dma((NQ, 2, ng)), dma((NQ, 2, NZ)), dma((NQ, 2, NZ)),
            dma((NQ, NZ)), dma((NQ, NZ)),
        ],
        compiler_params=pltpu.CompilerParams(
            collective_id=0, has_side_effects=True, vmem_limit_bytes=67043328),
    )(a_col, a_row, a_count, a_tiles, p_tiles)


def solution(mesh):
    in_specs = (
        P(("row", "col"), None, None),
        P(("row", "col")),
        P(("row", "col")),
        P(("row", "col")),
        P(("row", "col"), None, None),
    )
    out_specs = P(("row", "col"), None, None)
    return jax.shard_map(shards, mesh=mesh, in_specs=in_specs, out_specs=out_specs, check_vma=False)
```

```python
import functools

import jax
import jax.numpy as jnp
from jax import lax
from jax.experimental import pallas as pl
from jax.experimental.pallas import tpu as pltpu
from jax.sharding import PartitionSpec as P

MESH = pl.DeviceIdType.MESH
F32 = jnp.float32
BF16 = jnp.bfloat16
I32 = jnp.int32
NX, NZ, NQ = 4, 6, 2


def kernel_body(
    n_row, pb, slots, width,
    acol_h, arow_h, acount_h, a_hbm, p_hbm, out_ref,
    abuf, colbuf, row0, row1, img, seg0, seg1, tabv, tabs,
    fbuf, frecv, nbuf, nrecv, red, zb, zr,
    acol_s, arow_s, acount_s, acol_v, arow_v, s_sem,
    a_sem, p_sem, t_sem, sh_send, sh_recv,
    z_send, z_recv, x_send, x_recv, y_send, y_recv,
    f_send, f_recv, n_send, n_recv, q_send, q_recv,
):
    row = lax.axis_index("row")
    col = lax.axis_index("col")
    x = col // NZ
    z = lax.rem(col, NZ)
    core = lax.rem(row, 2)
    late = lax.rem(row // 2, 2)
    nc = 3 * pb
    rows = width // NQ
    rowb = (row0, row1)
    segs = (seg0, seg1)
    mate = (row + 1 - 2 * core, col)
    far = (lax.rem(row + n_row - 1 + 2 * core, n_row), col)
    mate_at = core * (2 * pb)
    far_at = (1 - core) * (2 * pb)
    xr = lax.rem(x + 1, NX)
    xl = lax.rem(x + NX - 1, NX)
    xf = lax.rem(x + 2, NX)
    right = (row, xr * NZ + z)
    left = (row, xl * NZ + z)
    has_up = z < NZ - 1
    has_dn = z > 0
    zup = (row, x * NZ + lax.rem(z + 1, NZ))
    zdn = (row, x * NZ + lax.rem(z + NZ - 1, NZ))

    def remote(src, dst, ssem, rsem, dev):
        return pltpu.make_async_remote_copy(
            src_ref=src, dst_ref=dst, send_sem=ssem, recv_sem=rsem,
            device_id=dev, device_id_type=MESH)

    def signal(dev):
        pl.semaphore_signal(pltpu.get_barrier_semaphore(), inc=1, device_id=dev, device_id_type=MESH)

    own = colbuf.at[pl.ds(pb, pb)]
    p_copy = pltpu.make_async_copy(p_hbm, own, p_sem)
    p_copy.start()
    small = [
        pltpu.make_async_copy(src, dst, s_sem.at[i]) for i, (src, dst) in enumerate((
            (acol_h, acol_s), (arow_h, arow_s), (acount_h, acount_s),
            (acol_h, acol_v), (arow_h, arow_v)))]
    barrier = pltpu.get_barrier_semaphore()
    for dev in (right, left, mate):
        signal(dev)
    pl.when(has_up)(lambda: signal(zup))
    pl.when(has_dn)(lambda: signal(zdn))

    p_copy.wait()
    for k in range(pb):
        flipped = colbuf[pb + k].T
        for q in range(NQ):
            rowb[q][col * pb + k] = flipped[q * rows:(q + 1) * rows]

    near = 3 + has_up.astype(I32) + has_dn.astype(I32)
    pl.semaphore_wait(barrier, near + late)
    signal(far)

    half = pb // 2

    def z_msg(q, zz, h, dev):
        s = rowb[q].at[pl.ds((x * NZ + zz) * pb + h * half, half)]
        return remote(s, s, z_send.at[q, h, zz], z_recv.at[q, h, zz], dev)

    def z_both(q, side, h):
        s = rowb[q].at[pl.ds(col * pb + h * half, half)]
        return remote(s, s, z_send.at[q, h, NZ + side], z_recv.at[q, h, z], zup if side == 0 else zdn)

    def x_msg(q, d, xx, zz):
        s = rowb[q].at[pl.ds((xx * NZ + zz) * pb, pb)]
        return remote(s, s, x_send.at[q, d, zz], x_recv.at[q, d, zz], right if d == 0 else left)

    def y_msg(q, d, xx, zz):
        s = rowb[q].at[pl.ds((xx * NZ + zz) * pb + d * half, half)]
        return remote(s, s, y_send.at[q, d, zz], y_recv.at[q, d, zz], right if d == 0 else left)

    pairs = jnp.minimum(z, NZ - 1 - z)
    more_below = z > NZ - 1 - z

    def place(n):
        if n == 0:
            return z
        side = (z - (n + 1) // 2) if n % 2 else (z + n // 2)
        rest = jnp.where(more_below, z - (n - pairs), z + (n - pairs))
        return jnp.where(n <= 2 * pairs, side, rest)

    def step(q, n):
        zz = place(n)
        for h in range(2):
            if n == 0:
                pl.when(has_up)(lambda h=h: z_both(q, 0, h).start())
                pl.when(has_dn)(lambda h=h: z_both(q, 1, h).start())
            else:
                z_msg(q, zz, h, zup).wait_recv()
                pl.when((zz < z) & has_up)(lambda h=h: z_msg(q, zz, h, zup).start())
                pl.when((zz > z) & has_dn)(lambda h=h: z_msg(q, zz, h, zdn).start())
        x_msg(q, 0, x, zz).start()
        x_msg(q, 1, x, zz).start()

    def relay(q, n):
        zz = place(n)
        x_msg(q, 0, xl, zz).wait_recv()
        y_msg(q, 0, xl, zz).start()
        x_msg(q, 1, xr, zz).wait_recv()
        y_msg(q, 1, xr, zz).start()

    def arrived(q):
        for n in range(NZ):
            zz = place(n)
            y_msg(q, 0, xf, zz).wait_recv()
            y_msg(q, 1, xf, zz).wait_recv()

    def drain(q):
        for h in range(2):
            pl.when(has_up)(lambda h=h: z_both(q, 0, h).wait_send())
            pl.when(has_dn)(lambda h=h: z_both(q, 1, h).wait_send())
        for n in range(NZ):
            zz = place(n)
            for h in range(2 if n > 0 else 0):
                pl.when((zz < z) & has_up)(lambda h=h, zz=zz: z_msg(q, zz, h, zup).wait_send())
                pl.when((zz > z) & has_dn)(lambda h=h, zz=zz: z_msg(q, zz, h, zdn).wait_send())
            for d in range(2):
                x_msg(q, d, x, zz).wait_send()
                y_msg(q, d, x, zz).wait_send()

    step(0, 0)
    to_mate = remote(own, colbuf.at[pl.ds(mate_at, pb)], sh_send.at[0], sh_recv.at[0], mate)
    to_far = remote(own, colbuf.at[pl.ds(far_at, pb)], sh_send.at[1], sh_recv.at[1], far)
    to_mate.start()
    step(1, 0)
    pl.when(late == 1)(lambda: to_far.start())

    n_a = 4
    part = slots // n_a
    a_copies = [
        pltpu.make_async_copy(
            a_hbm.at[pl.ds(i * part, part)], abuf.at[pl.ds(i * part, part)], a_sem.at[i])
        for i in range(n_a)]
    for c in small + a_copies:
        c.start()

    for c in small:
        c.wait()
    lane = lax.broadcasted_iota(I32, (slots, slots), 1)
    sub = lax.broadcasted_iota(I32, (slots, slots), 0)
    acol = jnp.broadcast_to(acol_v[...].reshape(1, slots), (slots, slots))
    arow = jnp.broadcast_to(arow_v[...].reshape(1, slots), (slots, slots))
    n_out = nc * pb
    key = jnp.where(lane < acount_s[0], (arow & (pb - 1)) * nc + acol, n_out)
    key_t = key.T
    before = (key_t < key) | ((key_t == key) & (sub < lane))
    rank = jnp.sum(before.astype(I32), axis=0, keepdims=True)
    rank_t = jnp.broadcast_to(rank, (slots, slots)).T
    hit = rank_t == lane
    order = jnp.sum(jnp.where(hit, sub, 0), axis=0, keepdims=True)
    s_key = jnp.sum(jnp.where(hit, key_t, 0), axis=0, keepdims=True)
    last = jnp.sum((key_t <= lane).astype(I32), axis=0, keepdims=True) - 1
    some = jnp.sum((key_t == lane).astype(I32), axis=0, keepdims=True)
    s_key8 = jnp.broadcast_to(s_key, (8, slots))
    prev = pltpu.roll(s_key8, 1, 1)
    lane8 = lax.broadcasted_iota(I32, (8, slots), 1)
    keep = jnp.where((lane8 > 0) & (prev == s_key8), 1, 0)
    sub8 = lax.broadcasted_iota(I32, (8, slots), 0)
    tabv[...] = jnp.where(
        sub8 == 0, jnp.broadcast_to(order, (8, slots)),
        jnp.where(sub8 == 1, keep,
                  jnp.where(sub8 == 2, jnp.broadcast_to(jnp.maximum(last, 0), (8, slots)),
                            jnp.broadcast_to(jnp.minimum(some, 1), (8, slots)))))
    t_copy = pltpu.make_async_copy(tabv, tabs, t_sem)
    t_copy.start()

    U = 32

    def images(first, count):
        def body(i, carry):
            for u in range(U):
                t = first + i * U + u
                img[t] = jnp.dot(abuf[t], colbuf[acol_s[t]],
                                 preferred_element_type=F32).astype(BF16)
            return carry
        lax.fori_loop(0, count // U, body, 0)

    def terms(q, first, count):
        def body(i, carry):
            for u in range(U):
                p = first + i * U + u
                t = tabs[0, p]
                term = jnp.dot(rowb[q][arow_s[t]], img[t], preferred_element_type=F32)
                carry = carry * tabs[1, p].astype(F32) + term
                segs[q][p] = carry
            return carry
        start = jnp.zeros((rows, width), F32) if first == 0 else segs[q][first - 1]
        lax.fori_loop(0, count // U, body, start)

    ct = nc // NZ

    def total(q, s):
        return segs[q][tabs[2, s]] * tabs[3, s].astype(F32)

    def group(d, i):
        return i if d == 0 else NZ - 1 - i

    def far_msg(q, d, i):
        return remote(fbuf.at[q, d, i], frecv.at[q, d, i], f_send.at[q, d, i], f_recv.at[q, d, i],
                      right if d == 0 else left)

    def near_msg(q, d, g):
        return remote(nbuf.at[q, d, g], nrecv.at[q, d, g], n_send.at[q, d, g], n_recv.at[q, d, g],
                      right if d == 0 else left)

    def z_out(q, g):
        return remote(zb.at[q, g], zr.at[q, z], q_send.at[q, g], q_recv.at[q, z], (row, x * NZ + g))

    def send_far(q, i):
        for d in range(2):
            for b in range(ct):
                fbuf[q, d, i, b] = total(q, xf * nc + group(d, i) * ct + b).astype(BF16)
            far_msg(q, d, i).start()

    def send_near(q, i):
        for d in range(2):
            g = group(1 - d, i)
            for b in range(ct):
                nbuf[q, d, g, b] = total(q, (xr if d == 0 else xl) * nc + g * ct + b).astype(BF16)
            near_msg(q, d, g).start()

    def send_joint(q, i):
        for d in range(2):
            g = group(d, i)
            far_msg(q, d, i).wait_recv()
            for b in range(ct):
                v = total(q, (xr if d == 0 else xl) * nc + g * ct + b)
                nbuf[q, d, g, b] = (v + frecv[q, d, i, b].astype(F32)).astype(BF16)
            near_msg(q, d, g).start()

    def finish(q, i):
        for g in (group(0, i), group(1, i)):
            near_msg(q, 0, g).wait_recv()
            near_msg(q, 1, g).wait_recv()
            for b in range(ct):
                v = total(q, x * nc + g * ct + b)
                v = v + nrecv[q, 0, g, b].astype(F32) + nrecv[q, 1, g, b].astype(F32)
                zb[q, g, b] = v.astype(BF16)

                def keep_own(v=v, b=b):
                    red[q, b] = v
                pl.when(z == g)(keep_own)
            pl.when(z != g)(lambda g=g: z_out(q, g).start())

    def z_in(q, zz):
        return remote(zb.at[q, 0], zr.at[q, zz], q_send.at[q, 0], q_recv.at[q, zz], zup)

    def close(q):
        for d in range(1, NZ):
            z_in(q, lax.rem(z + d, NZ)).wait_recv()
        for b in range(ct):
            v = red[q, b]
            for d in range(1, NZ):
                v = v + zr[q, lax.rem(z + d, NZ), b].astype(F32)
            out_ref[b, pl.ds(q * rows, rows)] = v.astype(BF16)

    def far_start():
        pl.semaphore_wait(barrier, 1)
        to_far.start()

    for n in range(1, NZ):
        step(0, n)
        step(1, n)
        if n >= 2:
            relay(0, n - 2)
            relay(1, n - 2)
        if n == NZ - 2:
            pl.when(late == 0)(far_start)
    to_mate.wait_recv()
    to_far.wait_recv()
    for c in a_copies:
        c.wait()
    quarter = slots // 4
    for i, (n, q) in enumerate([(NZ - 2, 0), (NZ - 2, 1), (NZ - 1, 0), (NZ - 1, 1)]):
        images(i * quarter, quarter)
        if i < 3:
            relay(q, n)
    t_copy.wait()
    arrived(0)
    terms(0, 0, slots // 2)
    relay(1, NZ - 1)
    terms(0, slots // 2, slots // 2)
    for i in range(NZ // 2):
        send_far(0, i)
    for i in range(NZ // 2):
        send_near(0, i)
    arrived(1)
    terms(1, 0, slots // 2)
    for i in range(NZ // 2):
        send_joint(0, i)
    terms(1, slots // 2, slots // 2)
    for i in range(NZ // 2):
        send_far(1, i)
    for i in range(NZ // 2):
        send_near(1, i)
    for i in range(NZ // 2):
        finish(0, i)
    for i in range(NZ // 2):
        send_joint(1, i)
    close(0)
    for i in range(NZ // 2):
        finish(1, i)
    close(1)

    to_mate.wait_send()
    to_far.wait_send()
    for q in range(NQ):
        drain(q)
        for d in range(2):
            for i in range(NZ // 2):
                far_msg(q, d, i).wait_send()
            for g in range(NZ):
                near_msg(q, d, g).wait_send()
        for g in range(NZ):
            pl.when(z != g)(lambda g=g: z_out(q, g).wait_send())


def shards(a_tiles, a_row, a_col, a_count, p_tiles):
    slots, width = a_tiles.shape[0], a_tiles.shape[1]
    pb = p_tiles.shape[0]
    n_row = lax.axis_size("row")
    n_col = lax.axis_size("col")
    nc = 3 * pb
    ct = nc * pb // n_col
    tile = (width, width)
    part = (width // NQ, width)
    vm = pltpu.VMEM
    dma = pltpu.SemaphoreType.DMA
    vmem = pl.BlockSpec(memory_space=pltpu.VMEM)
    hbm = pl.BlockSpec(memory_space=pltpu.HBM)
    ng = NZ // 2
    return pl.pallas_call(
        functools.partial(kernel_body, n_row, pb, slots, width),
        out_shape=jax.ShapeDtypeStruct((ct,) + tile, BF16),
        in_specs=[hbm] * 5,
        out_specs=vmem,
        scratch_shapes=[
            vm((slots,) + tile, BF16),
            vm((nc,) + tile, BF16),
            vm((n_col * pb,) + part, BF16),
            vm((n_col * pb,) + part, BF16),
            vm((slots,) + tile, BF16),
            vm((slots,) + part, F32),
            vm((slots,) + part, F32),
            vm((8, slots), I32),
            pltpu.SMEM((8, slots), I32),
            vm((NQ, 2, ng, ct) + part, BF16),
            vm((NQ, 2, ng, ct) + part, BF16),
            vm((NQ, 2, NZ, ct) + part, BF16),
            vm((NQ, 2, NZ, ct) + part, BF16),
            vm((NQ, ct) + part, F32),
            vm((NQ, NZ, ct) + part, BF16),
            vm((NQ, NZ, ct) + part, BF16),
            pltpu.SMEM((slots,), I32), pltpu.SMEM((slots,), I32), pltpu.SMEM((1,), I32),
            vm((slots,), I32), vm((slots,), I32), dma((5,)),
            dma((4,)), dma(()), dma(()), dma((2,)), dma((2,)),
            dma((NQ, 2, NZ + 2)), dma((NQ, 2, NZ)),
            dma((NQ, 2, NZ)), dma((NQ, 2, NZ)), dma((NQ, 2, NZ)), dma((NQ, 2, NZ)),
            dma((NQ, 2, ng)), dma((NQ, 2, ng)), dma((NQ, 2, NZ)), dma((NQ, 2, NZ)),
            dma((NQ, NZ)), dma((NQ, NZ)),
        ],
        compiler_params=pltpu.CompilerParams(
            collective_id=0, has_side_effects=True, vmem_limit_bytes=67043328),
    )(a_col, a_row, a_count, a_tiles, p_tiles)


def solution(mesh):
    in_specs = (
        P(("row", "col"), None, None),
        P(("row", "col")),
        P(("row", "col")),
        P(("row", "col")),
        P(("row", "col"), None, None),
    )
    out_specs = P(("row", "col"), None, None)
    return jax.shard_map(shards, mesh=mesh, in_specs=in_specs, out_specs=out_specs, check_vma=False)
```
